32 devices in a mesh: energy: 16 (over z, y, x), slab: 2 (over core).
Axes of the slice: x: 2, y: 2, z: 4, core: 2. Of those that a mesh axis runs over, the one named last changes fastest.
Arguments:
- green_free: bfloat16 [16, 2, 2, 256, 256], P('energy', 'slab')
- coupling: bfloat16 [2, 2, 256, 256], P('slab'), may hold values from -0.25 to 0.25
- screened: bfloat16 [8, 2, 2, 256, 256], P(None, 'slab'), may hold values from -6 to 6
- shift_offsets: int32 [8], replicated, may hold values from -1 to 1, as said below
Outputs:
- green: bfloat16 [16, 2, 2, 256, 256], P('energy', 'slab')
- sigma: float32 [16, 2, 2, 256, 256], P('energy', 'slab')
The draws below stay inside these ranges and needn't reach their ends.
Inputs may be any that keep to these rules, and one draw needn't show every extreme that they name: `shift_offsets`: offsets lie within one device's energy points on either side; both ends, -1 and 1, occur in every draw.
All inputs are finite; a program needn't handle non-finite values.
Results may differ from the reference program's by a relative error of at most 0.0061.
Values may be sent and summed in bfloat16 or wider, within the bound.
No kernel may reach another device: no remote copies, remote signals or barrier semaphores. Data moves between devices by JAX's collectives and lax.ppermute only.
A program may use at most 64 MiB of HBM per device.

```python
import math
import jax
import jax.numpy as jnp
from jax import lax

ORB = 256
E_DEV = 1
SHIFTS = 8
NE = 16
NS = 2


def draw_green_free(key, part):
    first_key = jax.random.fold_in(key, 0)
    third_key = jax.random.fold_in(key, 2)
    shape = (NE, NS, 2, ORB, ORB)
    noise = jax.random.normal(first_key, shape, jnp.float32)
    diagonal = jax.random.uniform(third_key, (NE, NS, ORB), jnp.float32, 0.7, 1.3)
    noise = noise * (0.25 / math.sqrt(ORB))
    identity = jnp.eye(ORB, dtype=jnp.float32)
    real = noise[:, :, 0] + diagonal[..., None] * identity
    whole = jnp.stack([real, noise[:, :, 1]], axis=2)
    return whole.astype(jnp.bfloat16)


def draw_shift_offsets(key, part):
    value_key = jax.random.fold_in(key, 11)
    place_key = jax.random.fold_in(key, 23)
    values = jax.random.randint(value_key, (SHIFTS,), -E_DEV, E_DEV + 1, dtype=jnp.int32)
    places = jax.random.permutation(place_key, SHIFTS)
    values = values.at[places[0]].set(E_DEV).at[places[1]].set(-E_DEV)
    return values.astype(jnp.int32)


def block_scale(stream_key, extent, cuts, smallest, largest):
    level, own = 1.0, jax.random.fold_in(stream_key, 6)
    for axis_at, blocks in cuts:
        steps = jnp.exp(jax.random.uniform(jax.random.fold_in(own, axis_at), (blocks,), jnp.float32, smallest / len(cuts), largest / len(cuts)))
        level = level * jnp.repeat(steps, extent[axis_at] // blocks).reshape([-1 if axis == axis_at else 1 for axis in range(len(extent))])
    return level


def gaussian(key, shape, deviation, limit, cuts=(), kind=jnp.bfloat16):
    factor_of = block_scale(key, shape, cuts, -0.22, 0.18) if cuts else 1.0
    drawn = jax.random.normal(key, shape, jnp.float32) * deviation * factor_of
    return jnp.minimum(jnp.maximum(drawn, -limit), limit).astype(kind)


def setup_inputs(seed: int = 0) -> dict:
    key_list = jax.random.split(jax.random.key(seed), 5)
    green_free = draw_green_free(jax.random.fold_in(key_list[4], 71), 0)
    coupling = gaussian(key_list[1], (NS, 2, ORB, ORB), (5 * ORB // 2) ** -0.5, 0.25, ((0, 2),))
    screened = gaussian(key_list[2], (SHIFTS, NS, 2, ORB, ORB), 1.0, 6.0, ((1, 2),))
    shift_offsets = draw_shift_offsets(jax.random.fold_in(key_list[4], 71), 0)
    return dict(green_free=green_free, coupling=coupling, screened=screened, shift_offsets=shift_offsets)


def complex_product(first, second, form):
    first_re = first[..., 0, :, :].astype(jnp.float32)
    first_im = first[..., 1, :, :].astype(jnp.float32)
    second_re = second[..., 0, :, :].astype(jnp.float32)
    second_im = second[..., 1, :, :].astype(jnp.float32)
    real = jnp.einsum(form, first_re, second_re) - jnp.einsum(form, first_im, second_im)
    imag = jnp.einsum(form, first_re, second_im) + jnp.einsum(form, first_im, second_re)
    return jnp.stack([real, imag], axis=-3)


def adjoint(block):
    real = jnp.swapaxes(block[..., 0, :, :], -1, -2)
    imag = -jnp.swapaxes(block[..., 1, :, :], -1, -2)
    return jnp.stack([real, imag], axis=-3)


def reference(green_free, coupling, screened, shift_offsets):
    left_map = complex_product(green_free, coupling, "esij,sjk->esik").astype(jnp.bfloat16)
    right_map = complex_product(adjoint(coupling), green_free, "sij,esjk->esik").astype(jnp.bfloat16)

    def advance(carry, slab_data):
        left_slab, right_slab, free_slab = slab_data
        middle = complex_product(left_slab, carry, "eij,ejk->eik").astype(jnp.bfloat16)
        fresh = (free_slab.astype(jnp.float32) + complex_product(middle, right_slab, "eij,ejk->eik")).astype(jnp.bfloat16)
        return fresh, fresh

    start = jnp.zeros((green_free.shape[0],) + green_free.shape[2:], jnp.bfloat16)
    _, swept = lax.scan(advance, start, (jnp.moveaxis(left_map, 1, 0), jnp.moveaxis(right_map, 1, 0), jnp.moveaxis(green_free, 1, 0)))
    green = jnp.moveaxis(swept, 0, 1)
    real_sum = jnp.zeros(green.shape[:2] + green.shape[3:], jnp.float32)
    imag_sum = jnp.zeros(green.shape[:2] + green.shape[3:], jnp.float32)
    for shift_no in range(SHIFTS):
        moved = jnp.roll(green, shift_offsets[shift_no], axis=0).astype(jnp.float32)
        weight = screened[shift_no].astype(jnp.float32)
        moved_re = moved[:, :, 0]
        moved_im = moved[:, :, 1]
        weight_re = weight[None, :, 0]
        weight_im = weight[None, :, 1]
        real_sum = real_sum + moved_re * weight_re - moved_im * weight_im
        imag_sum = imag_sum + moved_re * weight_im + moved_im * weight_re
    sigma = jnp.stack([-imag_sum, real_sum], axis=2)
    return green, sigma
```

```python
import functools

import jax
import jax.numpy as jnp
from jax import lax
from jax.experimental import pallas as pl
from jax.experimental.pallas import tpu as pltpu
from jax.sharding import PartitionSpec as P


VMEM = pl.BlockSpec(memory_space=pltpu.VMEM)
HBM = pl.BlockSpec(memory_space=pltpu.HBM)
SMEM = pl.BlockSpec(memory_space=pltpu.SMEM)


def dot(a, b):
    return jnp.dot(a, b, preferred_element_type=jnp.float32)


def dot_t(a, b):
    return lax.dot_general(a, b, (((0,), (0,)), ((), ())), preferred_element_type=jnp.float32)


def times(a, b):
    return dot(a[0], b[0]) - dot(a[1], b[1]), dot(a[0], b[1]) + dot(a[1], b[0])


def load_kernel(slab_ref, free_hbm, coupling_hbm, free_ref, coupling_ref, left_ref, right_ref, sems):
    copies = [
        pltpu.make_async_copy(free_hbm, free_ref, sems.at[0]),
        pltpu.make_async_copy(coupling_hbm, coupling_ref, sems.at[1]),
    ]
    for copy in copies:
        copy.start()
    for copy in copies:
        copy.wait()
    maps_kernel(slab_ref, free_ref, coupling_ref, left_ref, right_ref)


def maps_kernel(slab_ref, free_ref, coupling_ref, left_ref, right_ref):
    @pl.when(slab_ref[0] > 0)
    def _():
        free = free_ref[0], free_ref[1]
        coupling = coupling_ref[0], coupling_ref[1]
        left = times(free, coupling)
        left_ref[0] = left[0].astype(left_ref.dtype)
        left_ref[1] = left[1].astype(left_ref.dtype)
        right_re = dot_t(coupling[0], free[0]) + dot_t(coupling[1], free[1])
        right_im = dot_t(coupling[0], free[1]) - dot_t(coupling[1], free[0])
        right_ref[0] = right_re.astype(right_ref.dtype)
        right_ref[1] = right_im.astype(right_ref.dtype)


def advance_kernel(step, slab_ref, before_ref, now_ref, left_ref, right_ref, green_ref):
    @pl.when(slab_ref[0] == step)
    def _():
        middle = times((left_ref[0], left_ref[1]), (before_ref[0], before_ref[1]))
        middle = middle[0].astype(jnp.bfloat16), middle[1].astype(jnp.bfloat16)
        added = times(middle, (right_ref[0], right_ref[1]))
        for part in range(2):
            fresh = now_ref[part].astype(jnp.float32) + added[part]
            green_ref[part] = fresh.astype(green_ref.dtype)

    @pl.when(slab_ref[0] != step)
    def _():
        green_ref[...] = now_ref[...]


def weights_kernel(place_ref, screened_ref, total_ref):
    total_ref[...] = jnp.zeros_like(total_ref)
    for shift in range(screened_ref.shape[0]):
        at = place_ref[shift]
        total_ref[at] += screened_ref[shift].astype(jnp.float32)


def add_products(pairs):
    real, imag = None, None
    for green, weight in pairs:
        green_re, green_im = green[0].astype(jnp.float32), green[1].astype(jnp.float32)
        one = green_re * weight[0] - green_im * weight[1]
        two = green_re * weight[1] + green_im * weight[0]
        real = one if real is None else real + one
        imag = two if imag is None else imag + two
    return real, imag


def near_kernel(own_ref, near_ref, total_ref, sum_ref):
    real, imag = add_products(
        (((own_ref[0], own_ref[1]), (total_ref[0, 0], total_ref[0, 1])),
         ((near_ref[0], near_ref[1]), (total_ref[1, 0], total_ref[1, 1])))
    )
    sum_ref[0] = -imag
    sum_ref[1] = real


def far_kernel(sum_ref, far_ref, total_ref, sigma_ref):
    real, imag = add_products((((far_ref[0], far_ref[1]), (total_ref[2, 0], total_ref[2, 1])),))
    sigma_ref[0] = sum_ref[0] - imag
    sigma_ref[1] = sum_ref[1] + real


PARAMS = pltpu.CompilerParams(vmem_limit_bytes=16 * 2**20)


def in_vmem(shape, dtype):
    return pltpu.VMEM(shape, dtype)


def shards(green_free, coupling, screened, shift_offsets):
    energies, slabs, parts, orbitals, _ = green_free.shape
    assert energies == 1 and slabs == 1
    count, segments = lax.axis_size("energy"), lax.axis_size("slab")
    block = (parts, orbitals, orbitals)
    free = green_free.reshape(block)
    coupled = coupling.reshape(block)
    weight = screened.reshape((screened.shape[0],) + block)
    slab = lax.axis_index("slab").astype(jnp.int32).reshape(1)

    if count % 2 == 0:
        first_pairs = [(e, (e + 1 if e % 2 else e - 1) % count) for e in range(count)]
        second_pairs = [(e, e ^ 1) for e in range(count)]
        toward = 1 - 2 * (lax.axis_index("energy") % 2)
    else:
        first_pairs = [(e, (e - 1) % count) for e in range(count)]
        second_pairs = [(e, (e + 1) % count) for e in range(count)]
        toward = -1
    place = jnp.where(shift_offsets == 0, 0, jnp.where(shift_offsets == toward, 1, 2))
    ring = [(s, (s + 1) % segments) for s in range(segments)]

    product = 8 * orbitals**3
    size = 2 * parts * orbitals * orbitals
    small = in_vmem(block, jnp.bfloat16)

    def cost(flops, arrays):
        return pl.CostEstimate(flops=flops, bytes_accessed=arrays * size, transcendentals=0)

    def swap(part):
        return lax.ppermute(part, "slab", ring)

    def advance(step, before, now, left, right):
        return pl.pallas_call(
            functools.partial(advance_kernel, step),
            out_shape=small,
            in_specs=[SMEM] + [VMEM] * 4,
            out_specs=VMEM,
            cost_estimate=cost(2 * product, 5),
            compiler_params=PARAMS,
        )(slab, before, now, left, right)

    before = swap(free)
    first_free = lax.ppermute(free, "energy", first_pairs)
    own, coupled, left, right = pl.pallas_call(
        load_kernel,
        out_shape=(small,) * 4,
        in_specs=[SMEM, HBM, HBM],
        out_specs=[VMEM] * 4,
        scratch_shapes=[pltpu.SemaphoreType.DMA((2,))],
        cost_estimate=cost(2 * product, 6),
        compiler_params=PARAMS,
    )(slab, free, coupled)
    green = own
    for step in range(1, segments):
        green = advance(step, before, green, left, right)
        if step < segments - 1:
            before = swap(green)
    second = lax.ppermute(green, "energy", second_pairs)
    total = pl.pallas_call(
        weights_kernel,
        out_shape=in_vmem((3,) + block, jnp.float32),
        in_specs=[SMEM, VMEM],
        out_specs=VMEM,
        cost_estimate=cost(0, screened.shape[0] + 6),
        compiler_params=PARAMS,
    )(place, weight)
    first = first_free
    before = swap(first)
    left, right = pl.pallas_call(
        maps_kernel,
        out_shape=(small,) * 2,
        in_specs=[SMEM, VMEM, VMEM],
        out_specs=[VMEM, VMEM],
        cost_estimate=cost(2 * product, 4),
        compiler_params=PARAMS,
    )(slab, first, coupled)
    for step in range(1, segments):
        first = advance(step, before, first, left, right)
        if step < segments - 1:
            before = swap(first)
    partial = pl.pallas_call(
        near_kernel,
        out_shape=in_vmem(block, jnp.float32),
        in_specs=[VMEM] * 3,
        out_specs=VMEM,
        cost_estimate=cost(0, 10),
        compiler_params=PARAMS,
    )(green, first, total)
    sigma = pl.pallas_call(
        far_kernel,
        out_shape=jax.ShapeDtypeStruct(block, jnp.float32),
        in_specs=[VMEM] * 3,
        out_specs=VMEM,
        cost_estimate=cost(0, 10),
        compiler_params=PARAMS,
    )(partial, second, total)
    shape = (energies, slabs) + block
    return green.reshape(shape), sigma.reshape(shape)


def solution(mesh):
    placed = (
        P("energy", "slab", None, None, None),
        P("slab", None, None, None),
        P(None, "slab", None, None, None),
        P(),
    )
    return jax.shard_map(
        shards,
        mesh=mesh,
        in_specs=placed,
        out_specs=(P("energy", "slab", None, None, None), P("energy", "slab", None, None, None)),
        check_vma=False,
    )
```

```python
import functools

import jax
import jax.numpy as jnp
from jax import lax
from jax.experimental import pallas as pl
from jax.experimental.pallas import tpu as pltpu
from jax.sharding import PartitionSpec as P


VMEM = pl.BlockSpec(memory_space=pltpu.VMEM)
HBM = pl.BlockSpec(memory_space=pltpu.HBM)
SMEM = pl.BlockSpec(memory_space=pltpu.SMEM)


def dot(a, b):
    return jnp.dot(a, b, preferred_element_type=jnp.float32)


def dot_t(a, b):
    return lax.dot_general(a, b, (((0,), (0,)), ((), ())), preferred_element_type=jnp.float32)


def times(a, b):
    return dot(a[0], b[0]) - dot(a[1], b[1]), dot(a[0], b[1]) + dot(a[1], b[0])


def load_kernel(slab_ref, free_hbm, coupling_hbm, free_ref, left_ref, right_ref, coupling_ref, sems):
    copies = [
        pltpu.make_async_copy(free_hbm, free_ref, sems.at[0]),
        pltpu.make_async_copy(coupling_hbm, coupling_ref, sems.at[1]),
    ]
    for copy in copies:
        copy.start()
    for copy in copies:
        copy.wait()
    write_maps(slab_ref, free_ref, coupling_ref, left_ref, right_ref)


def write_maps(slab_ref, free_ref, coupling_ref, left_ref, right_ref):
    @pl.when(slab_ref[0] > 0)
    def _():
        free = free_ref[0], free_ref[1]
        coupling = coupling_ref[0], coupling_ref[1]
        left = times(free, coupling)
        left_ref[0] = left[0].astype(left_ref.dtype)
        left_ref[1] = left[1].astype(left_ref.dtype)
        right_re = dot_t(coupling[0], free[0]) + dot_t(coupling[1], free[1])
        right_im = dot_t(coupling[0], free[1]) - dot_t(coupling[1], free[0])
        right_ref[0] = right_re.astype(right_ref.dtype)
        right_ref[1] = right_im.astype(right_ref.dtype)


def advance_kernel(step, slab_ref, before_ref, now_ref, left_ref, right_ref, green_ref):
    @pl.when(slab_ref[0] == step)
    def _():
        middle = times((left_ref[0], left_ref[1]), (before_ref[0], before_ref[1]))
        middle = middle[0].astype(jnp.bfloat16), middle[1].astype(jnp.bfloat16)
        added = times(middle, (right_ref[0], right_ref[1]))
        for part in range(2):
            fresh = now_ref[part].astype(jnp.float32) + added[part]
            green_ref[part] = fresh.astype(green_ref.dtype)

    @pl.when(slab_ref[0] != step)
    def _():
        green_ref[...] = now_ref[...]


def weights_kernel(offset_ref, toward_ref, screened_ref, green_ref, total_ref, green_hbm, sem):
    copy = pltpu.make_async_copy(green_ref, green_hbm, sem)
    copy.start()
    total_ref[...] = jnp.zeros_like(total_ref)
    for shift in range(screened_ref.shape[0]):
        offset = offset_ref[shift]
        at = jnp.where(offset == 0, 0, jnp.where(offset == toward_ref[0], 1, 2))
        total_ref[at] += screened_ref[shift].astype(jnp.float32)
    copy.wait()


def add_products(pairs):
    real, imag = None, None
    for green, weight in pairs:
        green_re, green_im = green[0].astype(jnp.float32), green[1].astype(jnp.float32)
        one = green_re * weight[0] - green_im * weight[1]
        two = green_re * weight[1] + green_im * weight[0]
        real = one if real is None else real + one
        imag = two if imag is None else imag + two
    return real, imag


def pick_kernel(slab_ref, one_ref, two_ref, out_ref):
    @pl.when(slab_ref[0] == 0)
    def _():
        out_ref[...] = one_ref[...]

    @pl.when(slab_ref[0] != 0)
    def _():
        out_ref[...] = two_ref[...]


def partial_kernel(slab_ref, own_ref, one_ref, two_ref, total_ref, sum_ref):
    def write(other_ref):
        real, imag = add_products(
            (((own_ref[0], own_ref[1]), (total_ref[0, 0], total_ref[0, 1])),
             ((other_ref[0], other_ref[1]), (total_ref[1, 0], total_ref[1, 1])))
        )
        sum_ref[0] = -imag
        sum_ref[1] = real

    @pl.when(slab_ref[0] == 0)
    def _():
        write(one_ref)

    @pl.when(slab_ref[0] != 0)
    def _():
        write(two_ref)


CHUNKS = 4


def far_kernel(sum_ref, far_ref, total_ref, sigma_hbm, sigma_ref, sems):
    rows = far_ref.shape[1] // CHUNKS
    copies = []
    for chunk in range(CHUNKS):
        at = pl.ds(chunk * rows, rows)
        real, imag = add_products((((far_ref[0, at], far_ref[1, at]), (total_ref[2, 0, at], total_ref[2, 1, at])),))
        sigma_ref[0, at] = sum_ref[0, at] - imag
        sigma_ref[1, at] = sum_ref[1, at] + real
        for part in range(2):
            copies.append(pltpu.make_async_copy(sigma_ref.at[part, at], sigma_hbm.at[part, at], sems.at[chunk, part]))
            copies[-1].start()
    for copy in copies:
        copy.wait()


PARAMS = pltpu.CompilerParams(vmem_limit_bytes=16 * 2**20)


def in_hbm(array):
    return pltpu.with_memory_space_constraint(array, pltpu.HBM)


def in_vmem(shape, dtype):
    return pltpu.VMEM(shape, dtype)


def shards(green_free, coupling, screened, shift_offsets):
    energies, slabs, parts, orbitals, _ = green_free.shape
    assert energies == 1 and slabs == 1
    count, segments = lax.axis_size("energy"), lax.axis_size("slab")
    block = (parts, orbitals, orbitals)
    free = green_free.reshape(block)
    coupled = coupling.reshape(block)
    weight = screened.reshape((screened.shape[0],) + block)
    slab = lax.axis_index("slab").astype(jnp.int32).reshape(1)

    after = [(e + 1) % count for e in range(count)]
    if count % 2 == 0:
        near = [e ^ 1 for e in range(count)]
        far = [(e + 1 if e % 2 else e - 1) % count for e in range(count)]
        onward = [(e - 2 if e % 2 else e + 2) % count for e in range(count)]
        toward_near = 2 * (lax.axis_index("energy") % 2) - 1
    else:
        near = after
        far = [(e - 1) % count for e in range(count)]
        onward = [(e - 2) % count for e in range(count)]
        toward_near = 1
    idle = [e ^ 2 for e in range(count)] if count % 4 == 0 else after
    toward = jnp.where(slab == 0, toward_near, -toward_near).astype(jnp.int32)

    def exchange(part, base, others):
        pairs = []
        for e in range(count):
            for s in range(segments):
                pairs.append((e * segments + s, (others if s else base)[e] * segments + s))
        return lax.ppermute(part, ("energy", "slab"), pairs)

    ring = [(s, (s + 1) % segments) for s in range(segments)]

    product = 8 * orbitals**3
    size = 2 * parts * orbitals * orbitals
    small = in_vmem(block, jnp.bfloat16)

    def cost(flops, arrays):
        return pl.CostEstimate(flops=flops, bytes_accessed=arrays * size, transcendentals=0)

    def swap(part):
        return lax.ppermute(part, "slab", ring)

    def advance(step, before, now, left, right):
        return pl.pallas_call(
            functools.partial(advance_kernel, step),
            out_shape=small,
            in_specs=[SMEM] + [VMEM] * 4,
            out_specs=VMEM,
            cost_estimate=cost(2 * product, 5),
            compiler_params=PARAMS,
        )(slab, before, now, left, right)

    before = swap(free)
    first = exchange(free, near, idle)
    own, left, right = pl.pallas_call(
        load_kernel,
        out_shape=(small,) * 3,
        in_specs=[SMEM, HBM, HBM],
        out_specs=[VMEM] * 3,
        scratch_shapes=[small, pltpu.SemaphoreType.DMA((2,))],
        cost_estimate=cost(2 * product, 6),
        compiler_params=PARAMS,
    )(slab, in_hbm(free), in_hbm(coupled))
    green = own
    for step in range(1, segments):
        green = advance(step, before, green, left, right)
        if step < segments - 1:
            before = swap(green)
    second = exchange(green, idle, far)
    payload = pl.pallas_call(
        pick_kernel,
        out_shape=small,
        in_specs=[SMEM, VMEM, VMEM],
        out_specs=VMEM,
        cost_estimate=cost(0, 3),
        compiler_params=PARAMS,
    )(slab, first, green)
    third = exchange(payload, onward, near)
    total, green_out = pl.pallas_call(
        weights_kernel,
        out_shape=(in_vmem((3,) + block, jnp.float32), jax.ShapeDtypeStruct(block, jnp.bfloat16)),
        in_specs=[SMEM, SMEM, VMEM, VMEM],
        out_specs=[VMEM, HBM],
        scratch_shapes=[pltpu.SemaphoreType.DMA],
        cost_estimate=cost(0, screened.shape[0] + 6),
        compiler_params=PARAMS,
    )(shift_offsets, toward, weight, green)
    partial = pl.pallas_call(
        partial_kernel,
        out_shape=in_vmem(block, jnp.float32),
        in_specs=[SMEM] + [VMEM] * 4,
        out_specs=VMEM,
        cost_estimate=cost(0, 10),
        compiler_params=PARAMS,
    )(slab, green, first, second, total)
    sigma = pl.pallas_call(
        far_kernel,
        out_shape=jax.ShapeDtypeStruct(block, jnp.float32),
        in_specs=[VMEM] * 3,
        out_specs=HBM,
        scratch_shapes=[in_vmem(block, jnp.float32), pltpu.SemaphoreType.DMA((CHUNKS, 2))],
        cost_estimate=cost(0, 10),
        compiler_params=PARAMS,
    )(partial, third, total)
    shape = (energies, slabs) + block
    return green_out.reshape(shape), sigma.reshape(shape)


def solution(mesh):
    placed = (
        P("energy", "slab", None, None, None),
        P("slab", None, None, None),
        P(None, "slab", None, None, None),
        P(),
    )
    return jax.shard_map(
        shards,
        mesh=mesh,
        in_specs=placed,
        out_specs=(P("energy", "slab", None, None, None), P("energy", "slab", None, None, None)),
        check_vma=False,
    )
```

```python
import functools

import jax
import jax.numpy as jnp
from jax import lax
from jax.experimental import pallas as pl
from jax.experimental.pallas import tpu as pltpu
from jax.sharding import PartitionSpec as P


VMEM = pl.BlockSpec(memory_space=pltpu.VMEM)
HBM = pl.BlockSpec(memory_space=pltpu.HBM)
SMEM = pl.BlockSpec(memory_space=pltpu.SMEM)


def dot(a, b):
    return jnp.dot(a, b, preferred_element_type=jnp.float32)


def dot_t(a, b):
    return lax.dot_general(a, b, (((0,), (0,)), ((), ())), preferred_element_type=jnp.float32)


def times(a, b):
    return dot(a[0], b[0]) - dot(a[1], b[1]), dot(a[0], b[1]) + dot(a[1], b[0])


def mark_kernel(slab_ref, out_ref):
    out_ref[0] = slab_ref[0]


def maps_kernel(slab_ref, free_ref, coupling_ref, left_ref, right_ref):
    @pl.when(slab_ref[0] > 0)
    def _():
        free = free_ref[0], free_ref[1]
        coupling = coupling_ref[0], coupling_ref[1]
        left = times(free, coupling)
        left_ref[0] = left[0].astype(left_ref.dtype)
        left_ref[1] = left[1].astype(left_ref.dtype)
        right_re = dot_t(coupling[0], free[0]) + dot_t(coupling[1], free[1])
        right_im = dot_t(coupling[0], free[1]) - dot_t(coupling[1], free[0])
        right_ref[0] = right_re.astype(right_ref.dtype)
        right_ref[1] = right_im.astype(right_ref.dtype)


def advance_kernel(step, slab_ref, before_ref, now_ref, left_ref, right_ref, green_ref):
    @pl.when(slab_ref[0] == step)
    def _():
        middle = times((left_ref[0], left_ref[1]), (before_ref[0], before_ref[1]))
        middle = middle[0].astype(jnp.bfloat16), middle[1].astype(jnp.bfloat16)
        added = times(middle, (right_ref[0], right_ref[1]))
        for part in range(2):
            fresh = now_ref[part].astype(jnp.float32) + added[part]
            green_ref[part] = fresh.astype(green_ref.dtype)

    @pl.when(slab_ref[0] != step)
    def _():
        green_ref[...] = now_ref[...]


def weights_kernel(offset_ref, toward_ref, screened_ref, green_ref, total_ref, green_hbm, sem):
    copy = pltpu.make_async_copy(green_ref, green_hbm, sem)
    copy.start()
    total_ref[...] = jnp.zeros_like(total_ref)
    for shift in range(screened_ref.shape[0]):
        offset = offset_ref[shift]
        at = jnp.where(offset == 0, 0, jnp.where(offset == toward_ref[0], 1, 2))
        total_ref[at] += screened_ref[shift].astype(jnp.float32)
    copy.wait()


def add_products(pairs):
    real, imag = None, None
    for green, weight in pairs:
        green_re, green_im = green[0].astype(jnp.float32), green[1].astype(jnp.float32)
        one = green_re * weight[0] - green_im * weight[1]
        two = green_re * weight[1] + green_im * weight[0]
        real = one if real is None else real + one
        imag = two if imag is None else imag + two
    return real, imag


def partial_kernel(slab_ref, own_ref, one_ref, two_ref, total_ref, sum_ref):
    def write(other_ref):
        real, imag = add_products(
            (((own_ref[0], own_ref[1]), (total_ref[0, 0], total_ref[0, 1])),
             ((other_ref[0], other_ref[1]), (total_ref[1, 0], total_ref[1, 1])))
        )
        sum_ref[0] = -imag
        sum_ref[1] = real

    @pl.when(slab_ref[0] == 0)
    def _():
        write(one_ref)

    @pl.when(slab_ref[0] != 0)
    def _():
        write(two_ref)


CHUNKS = 4


def far_kernel(sum_ref, far_ref, total_ref, sigma_hbm, sigma_ref, sems):
    rows = far_ref.shape[1] // CHUNKS
    copies = []
    for chunk in range(CHUNKS):
        at = pl.ds(chunk * rows, rows)
        real, imag = add_products((((far_ref[0, at], far_ref[1, at]), (total_ref[2, 0, at], total_ref[2, 1, at])),))
        sigma_ref[0, at] = sum_ref[0, at] - imag
        sigma_ref[1, at] = sum_ref[1, at] + real
        for part in range(2):
            copies.append(pltpu.make_async_copy(sigma_ref.at[part, at], sigma_hbm.at[part, at], sems.at[chunk, part]))
            copies[-1].start()
    for copy in copies:
        copy.wait()


PARAMS = pltpu.CompilerParams(vmem_limit_bytes=16 * 2**20)


def in_vmem(shape, dtype):
    return pltpu.VMEM(shape, dtype)


def shards(green_free, coupling, screened, shift_offsets):
    energies, slabs, parts, orbitals, _ = green_free.shape
    assert energies == 1 and slabs == 1
    count, segments = lax.axis_size("energy"), lax.axis_size("slab")
    block = (parts, orbitals, orbitals)
    free = green_free.reshape(block)
    coupled = coupling.reshape(block)
    weight = screened.reshape((screened.shape[0],) + block)
    slab = lax.axis_index("slab").astype(jnp.int32).reshape(1)

    after = [(e + 1) % count for e in range(count)]
    if count % 2 == 0:
        near = [e ^ 1 for e in range(count)]
        far = [(e + 1 if e % 2 else e - 1) % count for e in range(count)]
        toward_near = 2 * (lax.axis_index("energy") % 2) - 1
    else:
        near = after
        far = [(e - 1) % count for e in range(count)]
        toward_near = 1
    idle = [e ^ 2 for e in range(count)] if count % 4 == 0 else after
    toward = jnp.where(slab == 0, toward_near, -toward_near).astype(jnp.int32)

    def exchange(part, base, others):
        pairs = []
        for e in range(count):
            for s in range(segments):
                pairs.append((e * segments + s, (others if s else base)[e] * segments + s))
        return lax.ppermute(part, ("energy", "slab"), pairs)

    ring = [(s, (s + 1) % segments) for s in range(segments)]

    product = 8 * orbitals**3
    size = 2 * parts * orbitals * orbitals
    small = in_vmem(block, jnp.bfloat16)

    def cost(flops, arrays):
        return pl.CostEstimate(flops=flops, bytes_accessed=arrays * size, transcendentals=0)

    def swap(part):
        return lax.ppermute(part, "slab", ring)

    def advance(step, before, now, left, right):
        return pl.pallas_call(
            functools.partial(advance_kernel, step),
            out_shape=small,
            in_specs=[SMEM] + [VMEM] * 4,
            out_specs=VMEM,
            cost_estimate=cost(2 * product, 5),
            compiler_params=PARAMS,
        )(slab, before, now, left, right)

    def mark(value, flops):
        return pl.pallas_call(
            mark_kernel,
            out_shape=pltpu.SMEM((1,), jnp.int32),
            in_specs=[SMEM],
            out_specs=SMEM,
            cost_estimate=pl.CostEstimate(flops=flops, bytes_accessed=1024, transcendentals=0),
            compiler_params=PARAMS,
        )(value)

    slab = mark(slab, 2**29)
    before = swap(free)
    first = exchange(free, near, idle)
    slab = mark(slab, 2**31)
    left, right = pl.pallas_call(
        maps_kernel,
        out_shape=(small,) * 2,
        in_specs=[SMEM, VMEM, VMEM],
        out_specs=[VMEM] * 2,
        cost_estimate=cost(2 * product, 4),
        compiler_params=PARAMS,
    )(slab, free, coupled)
    own = free
    green = own
    for step in range(1, segments):
        green = advance(step, before, green, left, right)
        if step < segments - 1:
            before = swap(green)
    second = exchange(green, idle, far)
    third = exchange(green, far, near)
    total, green_out = pl.pallas_call(
        weights_kernel,
        out_shape=(in_vmem((3,) + block, jnp.float32), jax.ShapeDtypeStruct(block, jnp.bfloat16)),
        in_specs=[SMEM, SMEM, VMEM, VMEM],
        out_specs=[VMEM, HBM],
        scratch_shapes=[pltpu.SemaphoreType.DMA],
        cost_estimate=cost(0, screened.shape[0] + 6),
        compiler_params=PARAMS,
    )(shift_offsets, toward, weight, green)
    partial = pl.pallas_call(
        partial_kernel,
        out_shape=in_vmem(block, jnp.float32),
        in_specs=[SMEM] + [VMEM] * 4,
        out_specs=VMEM,
        cost_estimate=cost(0, 10),
        compiler_params=PARAMS,
    )(slab, green, first, second, total)
    sigma = pl.pallas_call(
        far_kernel,
        out_shape=jax.ShapeDtypeStruct(block, jnp.float32),
        in_specs=[VMEM] * 3,
        out_specs=HBM,
        scratch_shapes=[in_vmem(block, jnp.float32), pltpu.SemaphoreType.DMA((CHUNKS, 2))],
        cost_estimate=cost(0, 10),
        compiler_params=PARAMS,
    )(partial, third, total)
    shape = (energies, slabs) + block
    return green_out.reshape(shape), sigma.reshape(shape)


def solution(mesh):
    placed = (
        P("energy", "slab", None, None, None),
        P("slab", None, None, None),
        P(None, "slab", None, None, None),
        P(),
    )
    return jax.shard_map(
        shards,
        mesh=mesh,
        in_specs=placed,
        out_specs=(P("energy", "slab", None, None, None), P("energy", "slab", None, None, None)),
        check_vma=False,
    )
```
